32 devices in a mesh: gx: 8 (over y, x, core), gy: 4 (over z).
Axes of the slice: x: 2, y: 2, z: 4, core: 2. Of those that a mesh axis runs over, the one named last changes fastest.
Arguments:
- thinker_normed: bfloat16 [4, 16, 8192], P(None, None, 'gx'), may hold values from -6 to 6
- thinker_resid: bfloat16 [4, 16, 8192], P('gy', None, 'gx'), may hold values from -6 to 6
- gate_weight: bfloat16 [8192, 29568], P('gx', 'gy'), may hold values from -0.0625 to 0.0625
- up_weight: bfloat16 [8192, 29568], P('gx', 'gy'), may hold values from -0.0625 to 0.0625
- down_weight: bfloat16 [29568, 8192], P('gy', 'gx'), may hold values from -0.03125 to 0.03125
- bridge_weight: bfloat16 [8192, 3584], P('gx'), may hold values from -0.0625 to 0.0625
- talker_stream: bfloat16 [4, 1536, 3584], P('gy', 'gx'), may hold values from -6 to 6
- norm_gain: float32 [3584], replicated, may hold values from 0.5 to 2
- w_query: bfloat16 [3584, 1792], P(None, 'gy'), may hold values from -0.09375 to 0.09375
- w_key: bfloat16 [3584, 256], P(None, 'gy'), may hold values from -0.09375 to 0.09375
- w_value: bfloat16 [3584, 256], P(None, 'gy'), may hold values from -0.09375 to 0.09375
- a_query: bfloat16 [3584, 64], replicated, may hold values from -0.09375 to 0.09375
- b_query: bfloat16 [64, 1792], replicated, may hold values from -0.75 to 0.75
- a_value: bfloat16 [3584, 64], replicated, may hold values from -0.09375 to 0.09375
- b_value: bfloat16 [64, 256], replicated, may hold values from -0.75 to 0.75
- text_index: int32 [4, 1536], P('gy', 'gx'), may hold values from 0 to 15
- span_offset: int32 [4], P('gy'), may hold values from 1 to 1535
- out_grad: bfloat16 [4, 1536, 1792], P('gy', 'gx'), may hold values from -6 to 6
Outputs:
- attn_out: bfloat16 [4, 1536, 1792], P('gy', 'gx')
- grad_aq: float32 [3584, 64], replicated
- grad_bq: float32 [64, 1792], replicated
- grad_av: float32 [3584, 64], replicated
- grad_bv: float32 [64, 256], replicated
The draws below stay inside these ranges and needn't reach their ends.
All inputs are finite; a program needn't handle non-finite values.
Results may differ from the reference program's by a relative error of at most 0.035.
Values may be sent and summed in bfloat16 or wider, within the bound.
No kernel may reach another device: no remote copies, remote signals or barrier semaphores. Data moves between devices by JAX's collectives and lax.ppermute only.
A program may use at most 192 MiB of HBM per device.

```python
import math
import jax
import jax.numpy as jnp
from jax import lax

DT = 8192
FF = 29568
DM = 3584
HEADS = 14
KVH = 2
HD = 128
RANK = 64
R_SEQ = 16
LEN = 1536
SEQS = 4


def draw_norm_gain(key, part):
    return jax.random.uniform(key, (DM,), jnp.float32, 0.5, 1.5)


def set_ends(result, stream_key, smallest, high):
    longest = result.shape.index(max(result.shape))
    spots = []
    for shift in (0, 1):
        where = [jax.random.randint(jax.random.fold_in(stream_key, axis), (), 0, length) for axis, length in enumerate(result.shape)]
        where[longest] = (where[longest] + shift) % result.shape[longest]
        spots.append(tuple(where))
    return result.at[spots[0]].set(smallest).at[spots[1]].set(high)


def levels(rng, extent, shards, smallest, top_value):
    gain = 1.0
    for dim, parts in shards:
        steps = jax.random.uniform(jax.random.fold_in(jax.random.fold_in(rng, 6), dim), (parts,), jnp.float32, smallest / len(shards), top_value / len(shards))
        gain = gain * jnp.repeat(jnp.exp(steps), extent[dim] // parts).reshape((-1,) + (1,) * (len(extent) - 1 - dim))
    return gain


def noise(rng, dims, deviation, most, split=(), held_as=jnp.bfloat16):
    loudness = levels(rng, dims, split, -0.22, 0.18) if split else 1.0
    drawn = jax.random.normal(rng, dims, jnp.float32) * deviation * loudness
    return jnp.minimum(jnp.maximum(drawn, -most), most).astype(held_as)


def setup_inputs(seed: int = 0) -> dict:
    arg_keys = jax.random.split(jax.random.key(seed), 19)
    thinker_normed = noise(arg_keys[0], (SEQS, R_SEQ, DT), 1.0, 6.0, ((2, 8),))
    thinker_resid = noise(arg_keys[1], (SEQS, R_SEQ, DT), 1.0, 6.0, ((0, 4), (2, 8)))
    gate_weight = noise(arg_keys[2], (DT, FF), DT ** -0.5, 0.0625, ((0, 8), (1, 4)))
    up_weight = noise(arg_keys[3], (DT, FF), DT ** -0.5, 0.0625, ((0, 8), (1, 4)))
    down_weight = noise(arg_keys[4], (FF, DT), FF ** -0.5, 0.03125, ((0, 4), (1, 8)))
    bridge_weight = noise(arg_keys[5], (DT, DM), DT ** -0.5, 0.0625, ((0, 8),))
    talker_stream = noise(arg_keys[6], (SEQS, LEN, DM), 1.0, 6.0, ((0, 4), (1, 8)))
    norm_gain = draw_norm_gain(jax.random.fold_in(arg_keys[18], 71), 0)
    w_query = noise(arg_keys[8], (DM, HEADS * HD), DM ** -0.5, 0.09375, ((1, 4),))
    w_key = noise(arg_keys[9], (DM, KVH * HD), DM ** -0.5, 0.09375, ((1, 4),))
    w_value = noise(arg_keys[10], (DM, KVH * HD), DM ** -0.5, 0.09375, ((1, 4),))
    a_query = noise(arg_keys[11], (DM, RANK), DM ** -0.5, 0.09375)
    b_query = noise(arg_keys[12], (RANK, HEADS * HD), RANK ** -0.5, 0.75)
    a_value = noise(arg_keys[13], (DM, RANK), DM ** -0.5, 0.09375)
    b_value = noise(arg_keys[14], (RANK, KVH * HD), RANK ** -0.5, 0.75)
    text_index = set_ends(jax.random.randint(arg_keys[15], (SEQS, LEN), 0, R_SEQ), jax.random.fold_in(arg_keys[15], 1), 0, R_SEQ - 1).astype(jnp.int32)
    span_offset = set_ends(jax.random.randint(arg_keys[16], (SEQS,), 1, LEN), jax.random.fold_in(arg_keys[16], 1), 1, LEN - 1).astype(jnp.int32)
    out_grad = noise(arg_keys[17], (SEQS, LEN, HEADS * HD), 1.0, 6.0, ((0, 4), (1, 8)))
    return dict(thinker_normed=thinker_normed, thinker_resid=thinker_resid, gate_weight=gate_weight, up_weight=up_weight, down_weight=down_weight, bridge_weight=bridge_weight, talker_stream=talker_stream, norm_gain=norm_gain, w_query=w_query, w_key=w_key, w_value=w_value, a_query=a_query, b_query=b_query, a_value=a_value, b_value=b_value, text_index=text_index, span_offset=span_offset, out_grad=out_grad)


rope_base = 1000000.0
norm_eps = 1e-06

def angle_tables(first_pos, length):
    position = (first_pos + jnp.arange(length, dtype=jnp.int32)).astype(jnp.float32)
    frequency = rope_base ** (-(2.0 * jnp.arange(HD // 2, dtype=jnp.float32)) / HD)
    angles = position[:, None] * frequency[None, :]
    return (jnp.cos(angles), jnp.sin(angles))

def rotate(tensor, cosine, sine_table, signed):
    layout = (cosine.shape[0],) + (1,) * (tensor.ndim - 2) + (cosine.shape[1],)
    cosine = cosine.reshape(layout)
    sine_part = sine_table.reshape(layout) * signed
    half_width = tensor.shape[-1] // 2
    first_half = tensor[..., :half_width]
    second_half = tensor[..., half_width:]
    return jnp.concatenate([first_half * cosine - second_half * sine_part, second_half * cosine + first_half * sine_part], axis=-1)

def reference(thinker_normed, thinker_resid, gate_weight, up_weight, down_weight, bridge_weight, talker_stream, norm_gain, w_query, w_key, w_value, a_query, b_query, a_value, b_value, text_index, span_offset, out_grad):
    normed = thinker_normed.reshape(SEQS * R_SEQ, DT)
    gate_part = jnp.dot(normed, gate_weight, preferred_element_type=jnp.float32)
    up_part = jnp.dot(normed, up_weight, preferred_element_type=jnp.float32)
    hidden = (jax.nn.silu(gate_part) * up_part).astype(jnp.bfloat16)
    thinker_out = (jnp.dot(hidden, down_weight, preferred_element_type=jnp.float32) + thinker_resid.reshape(SEQS * R_SEQ, DT).astype(jnp.float32)).astype(jnp.bfloat16)
    bridge = jnp.dot(thinker_out, bridge_weight, preferred_element_type=jnp.float32).astype(jnp.bfloat16).reshape(SEQS, R_SEQ, DM)
    groups = HEADS // KVH
    scale = 1.0 / math.sqrt(HD)

    def one_sequence(inputs):
        stream, picks, table, offset, cotangent = inputs
        length = stream.shape[0]
        mixed = stream.astype(jnp.float32) + table[picks].astype(jnp.float32)
        normal = (mixed * lax.rsqrt(lax.optimization_barrier(jnp.mean(mixed * mixed, axis=1, keepdims=True)) + norm_eps) * norm_gain).astype(jnp.bfloat16)
        low_query = jnp.dot(normal, a_query, preferred_element_type=jnp.float32).astype(jnp.bfloat16)
        low_value = jnp.dot(normal, a_value, preferred_element_type=jnp.float32).astype(jnp.bfloat16)
        cosine, sine_table = angle_tables(jnp.int32(0), length)
        query_pre = jnp.dot(normal, w_query, preferred_element_type=jnp.float32) + jnp.dot(low_query, b_query, preferred_element_type=jnp.float32)
        query = rotate(query_pre.reshape(length, KVH, groups, HD), cosine, sine_table, 1.0).astype(jnp.bfloat16)
        key_pre = jnp.dot(normal, w_key, preferred_element_type=jnp.float32).reshape(length, KVH, HD)
        key_rows = rotate(key_pre, cosine, sine_table, 1.0).astype(jnp.bfloat16)
        value_pre = jnp.dot(normal, w_value, preferred_element_type=jnp.float32) + jnp.dot(low_value, b_value, preferred_element_type=jnp.float32)
        value_rows = value_pre.astype(jnp.bfloat16).reshape(length, KVH, HD)
        places = jnp.arange(length, dtype=jnp.int32)
        causal = (places[None, :] <= places[:, None]) | (places[None, :] < offset)
        scores = jnp.einsum('tkgd,skd->kgts', query.astype(jnp.float32), key_rows.astype(jnp.float32)) * scale
        scores = jnp.where(causal, scores, -1e+30)
        row_max = lax.optimization_barrier(jnp.max(scores, axis=-1, keepdims=True))
        weights = jnp.exp(scores - row_max)
        probs = (weights / lax.optimization_barrier(jnp.sum(weights, axis=-1, keepdims=True))).astype(jnp.bfloat16)
        attended = jnp.einsum('kgts,skd->tkgd', probs.astype(jnp.float32), value_rows.astype(jnp.float32)).astype(jnp.bfloat16)
        grad_four = cotangent.reshape(length, KVH, groups, HD).astype(jnp.float32)
        inner_prod = lax.optimization_barrier(jnp.sum(grad_four * attended.astype(jnp.float32), axis=-1))
        dprob = jnp.einsum('tkgd,skd->kgts', grad_four, value_rows.astype(jnp.float32))
        dscore = (probs.astype(jnp.float32) * (dprob - jnp.transpose(inner_prod, (1, 2, 0))[..., None])).astype(jnp.bfloat16)
        dquery = jnp.einsum('kgts,skd->tkgd', dscore.astype(jnp.float32), key_rows.astype(jnp.float32)) * scale
        query_grad = rotate(dquery, cosine, sine_table, -1.0).reshape(length, HEADS * HD).astype(jnp.bfloat16)
        dvalue = jnp.einsum('kgts,tkgd->skd', probs.astype(jnp.float32), grad_four)
        value_grad = dvalue.reshape(length, KVH * HD).astype(jnp.bfloat16)
        grad_bq = jnp.dot(low_query.T, query_grad, preferred_element_type=jnp.float32)
        grad_bv = jnp.dot(low_value.T, value_grad, preferred_element_type=jnp.float32)
        dlow_query = jnp.dot(query_grad, b_query.T, preferred_element_type=jnp.float32).astype(jnp.bfloat16)
        dlow_value = jnp.dot(value_grad, b_value.T, preferred_element_type=jnp.float32).astype(jnp.bfloat16)
        grad_aq = jnp.dot(normal.T, dlow_query, preferred_element_type=jnp.float32)
        grad_av = jnp.dot(normal.T, dlow_value, preferred_element_type=jnp.float32)
        return (attended.reshape(length, HEADS * HD), grad_aq, grad_bq, grad_av, grad_bv)
    results = lax.map(one_sequence, (talker_stream, text_index, bridge, span_offset, out_grad))
    return (results[0], lax.optimization_barrier(jnp.sum(results[1], axis=0)), lax.optimization_barrier(jnp.sum(results[2], axis=0)), lax.optimization_barrier(jnp.sum(results[3], axis=0)), lax.optimization_barrier(jnp.sum(results[4], axis=0)))
```

```python
import math

import jax
import jax.numpy as jnp
from jax import lax
from jax.sharding import PartitionSpec as P

HEADS = 14
KVH = 2
HD = 128


rope_base = 1000000.0
norm_eps = 1e-06


def angle_tables(first_pos, length):
    position = (first_pos + jnp.arange(length, dtype=jnp.int32)).astype(jnp.float32)
    frequency = rope_base ** (-(2.0 * jnp.arange(HD // 2, dtype=jnp.float32)) / HD)
    angles = position[:, None] * frequency[None, :]
    return (jnp.cos(angles), jnp.sin(angles))


def rotate(tensor, cosine, sine_table, signed):
    layout = (cosine.shape[0],) + (1,) * (tensor.ndim - 2) + (cosine.shape[1],)
    cosine = cosine.reshape(layout)
    sine_part = sine_table.reshape(layout) * signed
    half_width = tensor.shape[-1] // 2
    first_half = tensor[..., :half_width]
    second_half = tensor[..., half_width:]
    return jnp.concatenate(
        [
            first_half * cosine - second_half * sine_part,
            second_half * cosine + first_half * sine_part,
        ],
        axis=-1,
    )


def bits_of(axis):
    size = lax.axis_size(axis)
    return [1 << k for k in range(size.bit_length() - 1)]


def swap(tensor, axis, distance):
    size = lax.axis_size(axis)
    return lax.ppermute(tensor, axis, [(i, i ^ distance) for i in range(size)])


def block_of(index, order):
    place = 0
    for bit in order:
        place = 2 * place + (index // bit) % 2
    return place


def blocks_by_place(tensor, order):
    count = 1 << len(order)
    rows = tensor.shape[0] // count
    owner = {block_of(i, order): i for i in range(count)}
    return jnp.concatenate([tensor[owner[p] * rows : (owner[p] + 1) * rows] for p in range(count)], axis=0)


def halve(tensor, axis, order):
    me = lax.axis_index(axis)
    for bit in order:
        rows = tensor.shape[0] // 2
        mine = (me // bit) % 2
        keep = lax.dynamic_slice_in_dim(tensor, mine * rows, rows, 0)
        send = lax.dynamic_slice_in_dim(tensor, (1 - mine) * rows, rows, 0)
        got = swap(send.astype(jnp.bfloat16), axis, bit)
        tensor = keep.astype(jnp.float32) + got.astype(jnp.float32)
    return tensor


def double(tensor, axis, order):
    me = lax.axis_index(axis)
    for bit in order:
        low = (me // bit) % 2 == 0
        got = swap(tensor, axis, bit)
        tensor = jnp.concatenate([jnp.where(low, tensor, got), jnp.where(low, got, tensor)], axis=0)
    return tensor


def add_all(tensor, axis, order):
    for bit in order:
        tensor = tensor.astype(jnp.bfloat16)
        tensor = tensor.astype(jnp.float32) + swap(tensor, axis, bit).astype(jnp.float32)
    return tensor


def dot(left, right):
    return jnp.dot(left, right, preferred_element_type=jnp.float32)


def on_device(
    thinker_normed,
    thinker_resid,
    gate_weight,
    up_weight,
    down_weight,
    bridge_weight,
    talker_stream,
    norm_gain,
    w_query,
    w_key,
    w_value,
    a_query,
    b_query,
    a_value,
    b_value,
    text_index,
    span_offset,
    out_grad,
):
    bf = jnp.bfloat16
    me_x = lax.axis_index("gx")
    me_y = lax.axis_index("gy")
    count_x = lax.axis_size("gx")
    count_y = lax.axis_size("gy")
    x_bits = bits_of("gx")
    order_a = x_bits
    order_b = x_bits[:1] + x_bits[:0:-1]
    seq_count, rows_seq, columns = thinker_normed.shape
    normed = thinker_normed.reshape(seq_count * rows_seq, columns)
    stream = talker_stream[0]
    tokens, width = stream.shape
    query_cols = w_query.shape[1]
    key_cols = w_key.shape[1]

    scaled = (stream.astype(jnp.float32) * norm_gain).astype(bf)
    scaled_other = swap(scaled, "gy", 1)
    half_width = width // 2
    piece_rows = half_width // count_x
    foreign = []
    pieces = []
    for which, order in enumerate((order_a, order_b)):
        start = which * half_width + block_of(me_x, order) * piece_rows
        pieces.append(
            jnp.concatenate(
                [lax.dynamic_slice_in_dim(w, start, piece_rows, 0) for w in (w_query, w_key, w_value)],
                axis=1,
            )
        )
    for distance in range(2, count_y, 2):
        foreign.append(
            [
                double(swap(piece, "gy", distance), "gx", order[::-1])
                for piece, order in zip(pieces, (order_a, order_b))
            ]
        )

    def project(rows):
        own = jnp.concatenate([dot(rows, w_query), dot(rows, w_key), dot(rows, w_value)], axis=1)
        out = [own.astype(bf)]
        for first, second in foreign:
            out.append((dot(rows[:, :half_width], first) + dot(rows[:, half_width:], second)).astype(bf))
        return jnp.stack(out)

    def in_order(blocks_even, blocks_odd):
        both = jnp.stack([blocks_even, blocks_odd], axis=1)
        both = both.reshape((count_y,) + both.shape[2:])
        return both[jnp.arange(count_y, dtype=jnp.int32) ^ me_y]

    early = project(jnp.concatenate([scaled, scaled_other], axis=0))
    early_back = swap(early[:, tokens:], "gy", 1)
    base = in_order(early[:, :tokens], early_back)

    gate_part = dot(blocks_by_place(normed, order_a), gate_weight).astype(bf)
    up_part = dot(blocks_by_place(normed, order_b), up_weight).astype(bf)
    gate_sum = halve(gate_part, "gx", order_a)
    up_sum = halve(up_part, "gx", order_b)
    hidden = (jax.nn.silu(gate_sum) * up_sum).astype(bf)
    hidden_all = lax.all_gather(hidden, "gx", axis=0, tiled=True)
    partial_out = dot(hidden_all, down_weight).astype(bf)
    summed = halve(partial_out, "gy", bits_of("gy")[::-1])
    thinker_out = (summed + thinker_resid[0].astype(jnp.float32)).astype(bf)
    bridge = add_all(dot(thinker_out, bridge_weight), "gx", x_bits).astype(bf)

    bridge_scaled = (bridge.astype(jnp.float32) * norm_gain).astype(bf)
    bridge_other = swap(bridge_scaled, "gy", 1)
    late = project(jnp.concatenate([bridge_scaled, bridge_other], axis=0))
    late_back = swap(late[:, rows_seq:], "gy", 1)
    late_all = in_order(late[:, :rows_seq], late_back)

    groups = HEADS // KVH
    scale = 1.0 / math.sqrt(HD)
    picks = (text_index[0][:, None] == jnp.arange(rows_seq, dtype=jnp.int32)[None, :]).astype(bf)
    mixed = stream.astype(jnp.float32) + dot(picks, bridge)
    inverse = lax.rsqrt(jnp.mean(mixed * mixed, axis=1, keepdims=True) + norm_eps)
    normal = (mixed * inverse * norm_gain).astype(bf)
    low_query = dot(normal, a_query).astype(bf)
    low_value = dot(normal, a_value).astype(bf)
    low_value_all = double(low_value, "gx", order_a[::-1])

    def columns_of(first, size):
        early_part = jnp.transpose(base[:, :, first : first + size], (1, 0, 2)).reshape(tokens, -1)
        late_part = jnp.transpose(late_all[:, :, first : first + size], (1, 0, 2)).reshape(rows_seq, -1)
        return (early_part.astype(jnp.float32) + dot(picks, late_part)) * inverse

    base_query = columns_of(0, query_cols)
    base_key = columns_of(query_cols, key_cols)
    base_value = columns_of(query_cols + key_cols, key_cols)
    first_pos = me_x * tokens
    cosine, sine_table = angle_tables(first_pos, tokens)
    query_pre = base_query + dot(low_query, b_query)
    query = rotate(query_pre.reshape(tokens, KVH, groups, HD), cosine, sine_table, 1.0).astype(bf)
    key_local = (
        rotate(base_key.reshape(tokens, KVH, HD), cosine, sine_table, 1.0)
        .astype(bf)
        .reshape(tokens, KVH * HD)
    )
    value_local = (base_value + dot(low_value, b_value)).astype(bf)
    keys_values = double(jnp.concatenate([key_local, value_local], axis=1), "gx", order_a[::-1])
    length = keys_values.shape[0]
    key_rows = keys_values[:, : KVH * HD].reshape(length, KVH, HD)
    value_rows = keys_values[:, KVH * HD :].reshape(length, KVH, HD)
    owner = {block_of(i, order_a): i for i in range(count_x)}
    key_places = jnp.concatenate(
        [owner[p] * tokens + jnp.arange(tokens, dtype=jnp.int32) for p in range(count_x)]
    )
    query_places = first_pos + jnp.arange(tokens, dtype=jnp.int32)
    causal = (key_places[None, :] <= query_places[:, None]) | (key_places[None, :] < span_offset[0])
    scores = (
        jnp.einsum("tkgd,skd->kgts", query, key_rows, preferred_element_type=jnp.float32) * scale
    )
    scores = jnp.where(causal, scores, -1e30)
    row_max = jnp.max(scores, axis=-1, keepdims=True)
    weights = jnp.exp(scores - row_max)
    probs = (weights / jnp.sum(weights, axis=-1, keepdims=True)).astype(bf)
    grad_four = out_grad[0].reshape(tokens, KVH, groups, HD)
    term = jnp.einsum("kgts,tkgd->skd", probs, grad_four, preferred_element_type=jnp.float32)
    term = term.reshape(length, KVH * HD).astype(bf)
    part_bv = jnp.einsum("tr,tc->rc", low_value_all, term, preferred_element_type=jnp.float32)
    part_low = jnp.einsum("tc,rc->tr", term, b_value, preferred_element_type=jnp.float32)
    dlow_value = halve(part_low, "gx", order_a).astype(bf)
    attended = jnp.einsum(
        "kgts,skd->tkgd", probs, value_rows, preferred_element_type=jnp.float32
    ).astype(bf)
    inner_prod = jnp.sum(grad_four.astype(jnp.float32) * attended.astype(jnp.float32), axis=-1)
    dprob = jnp.einsum("tkgd,skd->kgts", grad_four, value_rows, preferred_element_type=jnp.float32)
    dscore = (
        probs.astype(jnp.float32) * (dprob - jnp.transpose(inner_prod, (1, 2, 0))[..., None])
    ).astype(bf)
    dquery = (
        jnp.einsum("kgts,skd->tkgd", dscore, key_rows, preferred_element_type=jnp.float32) * scale
    )
    query_grad = (
        rotate(dquery, cosine, sine_table, -1.0).reshape(tokens, HEADS * HD).astype(bf)
    )
    part_bq = jnp.einsum("tr,tc->rc", low_query, query_grad, preferred_element_type=jnp.float32)
    dlow_query = jnp.einsum(
        "tc,rc->tr", query_grad, b_query, preferred_element_type=jnp.float32
    ).astype(bf)
    part_a = jnp.einsum(
        "td,tr->dr",
        normal,
        jnp.concatenate([dlow_query, dlow_value], axis=1),
        preferred_element_type=jnp.float32,
    )
    part_b = jnp.concatenate([part_bq, part_bv], axis=1)
    rank2 = part_a.shape[1]
    sum_first = halve(part_a[:half_width], "gx", order_a)
    sum_second = halve(part_a[half_width:], "gx", order_b)
    sum_b = halve(part_b, "gx", order_a)
    rows_b = sum_b.shape[0]
    packed = jnp.concatenate([sum_first, sum_second, sum_b.reshape(-1, rank2)], axis=0)
    packed = add_all(packed, "gy", bits_of("gy")).astype(bf)
    each = sum_first.shape[0]
    all_first = double(packed[:each], "gx", order_a[::-1])
    all_second = double(packed[each : 2 * each], "gx", order_b[::-1])
    all_b = double(packed[2 * each :].reshape(rows_b, -1), "gx", order_a[::-1]).astype(jnp.float32)
    grad_a = jnp.concatenate([all_first, all_second], axis=0).astype(jnp.float32)
    rank = a_query.shape[1]
    split = b_query.shape[1]
    attn_out = attended.reshape(1, tokens, HEADS * HD)
    return (attn_out, grad_a[:, :rank], all_b[:, :split], grad_a[:, rank:], all_b[:, split:])


def solution(mesh):
    return jax.shard_map(
        on_device,
        mesh=mesh,
        in_specs=(
            P(None, None, "gx"),
            P("gy", None, "gx"),
            P("gx", "gy"),
            P("gx", "gy"),
            P("gy", "gx"),
            P("gx", None),
            P("gy", "gx", None),
            P(),
            P(None, "gy"),
            P(None, "gy"),
            P(None, "gy"),
            P(),
            P(),
            P(),
            P(),
            P("gy", "gx"),
            P("gy"),
            P("gy", "gx", None),
        ),
        out_specs=(P("gy", "gx", None), P(), P(), P(), P()),
        check_vma=False,
    )
```
